256 devices in a mesh: tensor: 64 (over z_lo, x, y, core), dp: 4 (over z_hi).
Axes of the slice: x: 4, y: 4, z: 8 (z_hi: 4, z_lo: 2; z = z_hi * 2 + z_lo), core: 2. Of those that a mesh axis runs over, the one named last changes fastest.
Arguments:
- cotangent: bfloat16 [1024, 8192], P('dp', 'tensor'), may hold values from -12 to 12
- down_weight: bfloat16 [28672, 8192], P('tensor', 'dp'), may hold values from -0.0625 to 0.0625
- gate_pre: bfloat16 [1024, 28672], P('dp', 'tensor'), may hold values from -6 to 6
- up_pre: bfloat16 [1024, 28672], P('dp', 'tensor'), may hold values from -6 to 6
Outputs:
- factor: bfloat16 [64, 2, 33, 4, 50176], P('tensor', None, None, 'dp')
The draws below stay inside these ranges and needn't reach their ends.
All inputs are finite; a program needn't handle non-finite values.
Results may differ from the reference program's by a relative error of at most 0.0057.
Values may be sent and summed in bfloat16 or wider, within the bound.
A program may use at most 128 MiB of HBM per device.

```python
import math
import jax
import jax.numpy as jnp
from jax import lax

D = 8192
FF = 28672
TOKENS = 1024
N_TENSOR = 64
N_DP = 4


def draw_cotangent(key, part):
    value_key, spread_key = jax.random.split(jax.random.fold_in(key, 11))
    values = jnp.clip(jax.random.normal(value_key, (TOKENS, D), jnp.float32), -4.0, 4.0)
    spread = jnp.exp(jax.random.uniform(spread_key, (TOKENS, 1), jnp.float32, 0.0, math.log(10.0)))
    return (0.3 * values * spread).astype(jnp.bfloat16)


def level_of(stream_key, dims, cuts, smallest, largest):
    loudness = 1.0
    for position, blocks in cuts:
        draws = jax.random.uniform(jax.random.fold_in(jax.random.fold_in(stream_key, 6), position), (blocks,), jnp.float32, smallest / len(cuts), largest / len(cuts))
        loudness = loudness * jnp.repeat(jnp.exp(draws), dims[position] // blocks).reshape((-1,) + (1,) * (len(dims) - 1 - position))
    return loudness


def centred(stream_key, dims, deviation, bound, cuts=(), kind=jnp.bfloat16):
    array = deviation * jax.random.normal(stream_key, dims, jnp.float32)
    if cuts:
        array = array * level_of(stream_key, dims, cuts, -0.22, 0.18)
    return jnp.clip(array, -bound, bound).astype(kind)


def setup_inputs(seed: int = 0) -> dict:
    splits = jax.random.split(jax.random.key(seed), 5)
    return {
        "cotangent": draw_cotangent(jax.random.fold_in(splits[4], 71), 0),
        "down_weight": centred(splits[1], (FF, D), D ** -0.5, 0.0625, ((0, 64), (1, 4))),
        "gate_pre": centred(splits[2], (TOKENS, FF), 1.5, 6.0, ((0, 4), (1, 64))),
        "up_pre": centred(splits[3], (TOKENS, FF), 1.0, 6.0, ((0, 4), (1, 64))),
    }


def reference(cotangent, down_weight, gate_pre, up_pre):
    block_count = N_TENSOR
    block_width = FF // block_count
    band_width = block_count // 2 + 1
    slice_width = block_width // N_DP
    hidden_cot = jnp.dot(cotangent, down_weight.T, preferred_element_type=jnp.float32)
    gate_value = gate_pre.astype(jnp.float32)
    up_value = up_pre.astype(jnp.float32)
    sigmoid_gate = jax.nn.sigmoid(gate_value)
    grad_gate = (hidden_cot * up_value * sigmoid_gate * (1.0 + gate_value * (1.0 - sigmoid_gate))).astype(jnp.bfloat16)
    grad_up = (hidden_cot * gate_value * sigmoid_gate).astype(jnp.bfloat16)
    blocks = jnp.stack([grad_gate, grad_up]).reshape(2, TOKENS, block_count, block_width)

    def row_block(block_row):
        own_rows = lax.dynamic_index_in_dim(blocks, block_row, 2, keepdims=False).astype(jnp.float32)
        partner_index = ((block_row - jnp.arange(band_width).astype(jnp.int32)) % block_count).astype(jnp.int32)
        partner_cols = jnp.take(blocks, partner_index, axis=2).astype(jnp.float32)
        product = jnp.einsum("ftr,ftkc->fkrc", own_rows, partner_cols)
        tiles = (product * (1.0 / TOKENS)).astype(jnp.bfloat16)
        tiles = tiles.reshape(2, band_width, block_width, N_DP, slice_width)
        tiles = jnp.transpose(tiles, (0, 1, 3, 2, 4))
        return tiles.reshape(2, band_width, N_DP, block_width * slice_width)

    return lax.map(row_block, jnp.arange(block_count).astype(jnp.int32))
```

```python
import jax
import jax.numpy as jnp
from jax import lax
from jax.experimental import pallas as pl
from jax.experimental.pallas import tpu as pltpu
from jax.sharding import PartitionSpec as P

MESH = pl.DeviceIdType.MESH
NT = (((1,), (1,)), ((), ()))
F32 = jnp.float32
BF16 = jnp.bfloat16


def kernel(c_ref, w_ref, gate_ref, up_ref, y_ref,
           cq, hp, hf, hr, gu, rows, grouped, blocks, stage,
           s_send, s_cin, s_c, s_gu, s_h, s_rows, s_blk, s_loc):
    t = lax.axis_index("tensor")
    g = lax.axis_index("dp")
    core = t % 2
    y = (t // 2) % 4
    x = (t // 8) % 4
    zl = t // 32
    lt = c_ref.shape[0]
    sw = hp.shape[2]
    tokens = 4 * lt
    inv = 1.0 / tokens

    def tid(zz, xx, yy, cc):
        return ((zz * 4 + xx) * 4 + yy) * 2 + cc

    xp, xm = (x + 1) % 4, (x + 3) % 4
    yp, ym, y2 = (y + 1) % 4, (y + 3) % 4, (y + 2) % 4
    d_xp, d_xm = (tid(zl, xp, y, core), g), (tid(zl, xm, y, core), g)
    d_yp, d_ym = (tid(zl, x, yp, core), g), (tid(zl, x, ym, core), g)
    d_sib = (tid(zl, x, y, 1 - core), g)
    d_z = (tid(1 - zl, x, y, core), g)
    gp, gm, g2 = (g + 1) % 4, (g + 3) % 4, (g + 2) % 4
    d_gp, d_gm, d_g2 = (t, gp), (t, gm), (t, g2)
    d_zg = [(tid(1 - zl, x, y, core), q) for q in (gp, gm, g2)]

    barrier = pltpu.get_barrier_semaphore()
    friends = [d_xp, d_xm, d_yp, d_ym, d_sib, d_z, d_gp, d_gm, d_g2] + d_zg
    for d in friends:
        pl.semaphore_signal(barrier, inc=1, device_id=d, device_id_type=MESH)
    pl.semaphore_wait(barrier, len(friends))

    pending = []

    def send(src, dst, sem, dev, cond=None):
        copy = pltpu.make_async_remote_copy(
            src_ref=src, dst_ref=dst, send_sem=s_send.at[len(pending)], recv_sem=sem,
            device_id=dev, device_id_type=MESH)
        if cond is None:
            copy.start()
        else:
            pl.when(cond)(copy.start)
        pending.append((cond, copy))

    def arrived(ref, sem, cond=None):
        wait = pltpu.make_async_copy(ref, ref, sem).wait
        if cond is None:
            wait()
        else:
            pl.when(cond)(wait)

    home = t // 16
    slot = t % 16
    for p in range(2):
        me = (zl == p) & (home == g)
        dst = cq.at[g, slot]
        send(c_ref, dst, s_cin.at[g], (p * 32 + t % 32, home), jnp.logical_not(me))

        @pl.when(me)
        def _():
            own = pltpu.make_async_copy(c_ref, dst, s_loc)
            own.start()
            own.wait()

    def send_gate_up():
        for q, d in ((g2, d_g2), (gp, d_gp), (gm, d_gm)):
            for i, ref in enumerate((gate_ref, up_ref)):
                send(ref.at[pl.ds(q * sw, sw)], gu.at[i, g], s_gu.at[i, g], d)

    rel = (x + 4 - 2 * (g % 2)) % 4
    owner = rel < 2
    first = jnp.where((rel == 0) | (rel == 3), 0, 1)
    second = 1 - first

    def cslot(col, yy):
        return col * 8 + yy * 2 + core

    def c_send(q, j, dev, cond=None):
        send(cq.at[q, j], cq.at[q, j], s_c.at[q, j], dev, cond)

    def c_got(q, j, cond=None):
        arrived(cq.at[q, j], s_c.at[q, j], cond)

    def c_spread(q, j):
        c_send(q, j, d_yp)
        c_send(q, j, d_ym)
        c_send(q, j, d_sib)

    j1, j2 = cslot(first, y), cslot(second, y)

    def c0(q):
        mine = (zl == g // 2) & (g == q)
        arrived(cq.at[q, slot], s_cin.at[q], owner & jnp.logical_not(mine))
        c_got(q, j1, jnp.logical_not(owner))
        c_send(q, j1, d_xp, rel != 3)
        c_send(q, j1, d_xm, rel != 2)
        c_spread(q, j1)

    def c1(q):
        c_got(q, j2)
        c_spread(q, j2)

    def c_hop(q, col):
        j = cslot(col, ym)
        c_got(q, j)
        c_send(q, j, d_yp, col == 0)
        c_send(q, j, d_sib)
        j = cslot(col, yp)
        c_got(q, j)
        c_send(q, j, d_ym, col == 1)
        c_send(q, j, d_sib)

    def c2(q):
        c_hop(q, first)

    def c3(q):
        c_hop(q, second)

    def c4(q):
        for col in range(2):
            j = cslot(col, y2)
            c_got(q, j)
            c_send(q, j, d_sib)

    def partial(q):
        for i in range(8):
            c_got(q, i * 2 + 1 - core)
        right = jnp.concatenate([cq[q, j] for j in range(16)], axis=1)
        product = lax.dot_general(w_ref[...], right, NT, preferred_element_type=F32)
        for s in range(4):
            part = product[s * sw:(s + 1) * sw]
            hf[q, s] = part
            hp[s, q] = part.astype(BF16)
        for s, d in ((g2, d_g2), (gp, d_gp), (gm, d_gm)):
            send(hp.at[s, q], hr.at[g, q], s_h.at[g, q], d)

    def gradients(q):
        if q == 0:
            for s in (gp, gm, g2):
                for i in range(2):
                    arrived(gu.at[i, s], s_gu.at[i, s])
            own = pl.ds(pl.multiple_of(g * sw, 16), sw)
            gu[0, g] = gate_ref[own, :]
            gu[1, g] = up_ref[own, :]
        for s in (gp, gm, g2):
            arrived(hr.at[s, q], s_h.at[s, q])
        total = hf[q, g]
        for s in (gp, gm, g2):
            total = total + hr[s, q].astype(F32)
        gate = gu[0, q].astype(F32)
        up = gu[1, q].astype(F32)
        sig = jax.nn.sigmoid(gate)
        grads = (total * up * sig * (1.0 + gate * (1.0 - sig)), total * gate * sig)
        for f in range(2):
            value = grads[f].astype(BF16)
            rows[q, g, f] = value
            blocks[f, q, 0, 0:sw] = value

    def unit(q, m):
        return blocks.at[:, q, m, 0:sw]

    def pass_on(q, m_from, dev, m_to, cond=None):
        send(unit(q, m_from), unit(q, m_to), s_blk.at[q, m_to], dev, cond)

    def got(q, m, cond=None):
        arrived(unit(q, m), s_blk.at[q, m], cond)

    def to_sibling(q, m, cond=None):
        pass_on(q, m, d_sib, 17 if isinstance(m, int) and m == 16 else 18 + m, cond)

    def ahead(q, p):
        return (p != 2) if q % 2 == 0 else (p == 1)

    def behind(q, p):
        return (p == 2) if q % 2 == 0 else (p != 1)

    dyp, dym = yp - y, ym - y

    def rows_out(q):
        for d in (d_gp, d_gm):
            send(rows.at[q, g], rows.at[q, g], s_rows.at[q, g], d)

    def rows_on(q):
        for s, other, d in ((gm, 0, d_gp), (gp, 1, d_gm)):
            arrived(rows.at[q, s], s_rows.at[q, s])
            if q % 2 == other:
                send(rows.at[q, s], rows.at[q, s], s_rows.at[q, s], d)

    def b0(q):
        pass_on(q, 0, d_z, 16)
        pass_on(q, 0, d_xp, 4, x < 3)
        pass_on(q, 0, d_xm, 12, x == 0)
        pass_on(q, 0, d_yp, (dyp + 16) % 16, y < 3)
        pass_on(q, 0, d_ym, (dym + 16) % 16, y == 0)
        to_sibling(q, 0, core == 0)

    def b1(q):
        got(q, 16)
        pass_on(q, 16, d_xp, 4, x == 3)
        pass_on(q, 16, d_xm, 12, x > 0)
        pass_on(q, 16, d_yp, (dyp + 16) % 16, y == 3)
        pass_on(q, 16, d_ym, (dym + 16) % 16, y > 0)
        to_sibling(q, 16, core == 1)

    def spread_y(q, m):
        pass_on(q, m, d_yp, (m + dyp + 16) % 16)
        pass_on(q, m, d_ym, (m + dym + 16) % 16)
        to_sibling(q, m)

    def b2(q):
        got(q, 4)
        pass_on(q, 4, d_xp, 8, ahead(q, xm))
        spread_y(q, 4)
        got(q, 12)
        pass_on(q, 12, d_xm, 8, behind(q, xp))
        spread_y(q, 12)

    def b3(q):
        got(q, 8)
        spread_y(q, 8)

    def b4(base):
        def run(q):
            m = (base + y - ym + 16) % 16
            got(q, m)
            if base == 0:
                pass_on(q, m, d_yp, (m + dyp + 16) % 16, ahead(q, ym))
            elif q % 2 == 0:
                pass_on(q, m, d_yp, (m + dyp + 16) % 16)
            to_sibling(q, m)
            m = (base + y - yp + 16) % 16
            got(q, m)
            if base == 0:
                pass_on(q, m, d_ym, (m + dym + 16) % 16, behind(q, yp))
            elif q % 2 == 1:
                pass_on(q, m, d_ym, (m + dym + 16) % 16)
            to_sibling(q, m)
        return run

    def spare(d):
        return 33 + (d + 4) % 4

    def slot_o(d):
        return jnp.where(d > 0, d, spare(d))

    def slot_x(d):
        return jnp.where(d < 0, 16 + d, spare(d))

    def along_x(q, d):
        so, sx = slot_o(d), slot_x(d)
        pass_on(q, jnp.where(x < 3, so, sx), d_xp, (20 + d) % 16)
        pass_on(q, jnp.where(x == 0, so, sx), d_xm, (28 + d) % 16)

    def y0(q):
        pass_on(q, 0, d_z, 16)
        pass_on(q, 0, d_yp, slot_o(dyp))
        pass_on(q, 0, d_ym, slot_o(dym))
        pass_on(q, 0, d_xp, 4, x < 3)
        pass_on(q, 0, d_xm, 12, x == 0)
        to_sibling(q, 0, core == 0)

    def y1(q):
        got(q, 16)
        pass_on(q, 16, d_yp, slot_x(dyp))
        pass_on(q, 16, d_ym, slot_x(dym))
        pass_on(q, 16, d_xp, 4, x == 3)
        pass_on(q, 16, d_xm, 12, x > 0)
        to_sibling(q, 16, core == 1)

    def y_hop(q, source, dest, dev, forward):
        d = y - source
        for pick in (slot_o, slot_x):
            got(q, pick(d))
            if forward:
                pass_on(q, pick(d), dev, pick(dest - source))
        along_x(q, d)
        to_sibling(q, (d + 16) % 16)

    def y2a(q):
        y_hop(q, ym, yp, d_yp, q % 2 == 0)
        y_hop(q, yp, ym, d_ym, q % 2 == 1)

    def y3(q):
        y_hop(q, y2, None, None, False)

    def y4(source):
        def run(q):
            d = y - source
            m = (20 + d) % 16
            got(q, m)
            pass_on(q, m, d_xp, (24 + d) % 16, ahead(q, xm))
            to_sibling(q, m)
            m = (28 + d) % 16
            got(q, m)
            pass_on(q, m, d_xm, (24 + d) % 16, behind(q, xp))
            to_sibling(q, m)
        return run

    def y4b(q):
        y4(ym)(q)
        y4(yp)(q)

    def y5(q, source):
        m = (24 + y - source) % 16
        got(q, m)
        to_sibling(q, m)

    def start(q):
        gradients(q)
        (b0 if q < 2 else y0)(q)

    lead = [c0, c1, c2, c3, c4, partial]
    for wave in range(8):
        for q in range(4):
            if 0 <= wave - q < len(lead):
                lead[wave - q](q)
        if wave == 0:
            send_gate_up()
    start(0)
    partial(3)
    start(1)
    b1(0)
    start(2)
    b1(1)
    start(3)
    y1(2)
    y1(3)
    for q in range(4):
        rows_out(q)
    b2(0)
    y2a(2)
    b2(1)
    y2a(3)
    b3(0)
    b3(1)
    y3(2)
    y3(3)
    for q in range(4):
        (b4(0) if q < 2 else y4(y))(q)
    for q in range(4):
        rows_on(q)
    for base, late_y in ((4, y4b), (12, y4(y2)), (8, None)):
        for q in (0, 1):
            b4(base)(q)
        if late_y is not None:
            for q in (2, 3):
                late_y(q)
    for q in (2, 3):
        for source in (y, ym, yp):
            y5(q, source)
    for q in range(4):
        arrived(rows.at[q, g2], s_rows.at[q, g2])

    per_class = sw // 8
    target = lax.broadcasted_iota(jnp.int32, (128, sw), 0)
    source = lax.broadcasted_iota(jnp.int32, (128, sw), 1)
    pick = ((target % 16 < per_class) & (source == 8 * (target % 16) + target // 16)).astype(BF16)
    for f in range(2):
        for q in range(4):
            for s in range(4):
                moved = jnp.dot(pick, rows[q, s, f], preferred_element_type=F32)
                grouped[f, s, :, q * lt:(q + 1) * lt] = moved.astype(BF16)
    lane = lax.broadcasted_iota(jnp.int32, (16, 128), 1)

    def pair_of(i):
        late = jnp.where(i < 13, 2 * i - 17, 2 * i - 16)
        return jnp.where(i < 4, 2 * i, jnp.where(i < 5, 8, jnp.where(i < 9, 2 * i - 1, late)))

    def wanted(at):
        return jnp.where(core == 0, at != 18, at != 17)

    def place(at, half):
        k = jnp.where(at < 17, 2 * at, jnp.where(at == 17, 31, 2 * (at - 18) + 2 * core - 1))

        @pl.when(wanted(at))
        def _():
            y_ref[jnp.maximum(k, 0)] = stage[half, 0:y_ref.shape[1], :].astype(BF16)

    def step(i):
        p = pair_of(i)
        for f in range(2):
            left = grouped[f].reshape(512, tokens)
            right = jnp.concatenate(
                [blocks[f, q, pl.ds(2 * p, 2)].reshape(256, lt) for q in range(4)], axis=1)
            product = lax.dot_general(left, right, NT, preferred_element_type=F32)
            for half in range(2):
                tile = product[:, half * 128:half * 128 + 128] * inv
                for s in range(4):
                    turned = [
                        pltpu.roll(tile[s * 128 + r * 16:s * 128 + r * 16 + 16], (128 - 16 * r) % 128, 1)
                        for r in range(8)
                    ]
                    for r in range(7):
                        merged = jnp.where(lane < 112 - 16 * r, turned[r], turned[r + 1])
                        stage[half, pl.ds(14 * per_class * s + 2 * r + f, 16, stride=14), :] = merged
        for half in range(2):
            place(2 * p + half, half)

    base_index = len(pending)
    assert base_index + 8 <= s_send.shape[0], base_index

    def far(i, q):
        m = 4 * i + 2
        return pltpu.make_async_remote_copy(
            src_ref=unit(q, m), dst_ref=unit(q, 18 + m), send_sem=s_send.at[base_index + 2 * i + q],
            recv_sem=s_blk.at[q, 18 + m], device_id=d_sib, device_id_type=MESH)

    def from_sibling(m):
        for q in range(4):
            got(q, 18 + m)

    def early(i, _):
        @pl.when(i == 4)
        def _():
            for q in range(4):
                got(q, 17, core == 0)

        @pl.when((i > 5) | ((i == 5) & (core == 1)))
        def _():
            from_sibling(4 * (i - 5))

        @pl.when(i > 4)
        def _():
            from_sibling(4 * (i - 5) + 1)

        step(i)

        @pl.when(i < 4)
        def _():
            for q in range(2):
                got(q, 4 * i + 2)
                far(i, q).start()
        return 0

    def late(i, _):
        @pl.when(i > 12)
        def _():
            from_sibling(4 * (i - 13) + 2)
            from_sibling(4 * (i - 13) + 3)

        step(i)
        return 0

    lax.fori_loop(0, 9, early, 0)
    for q in (2, 3):
        y5(q, y2)
    lax.fori_loop(9, 17, late, 0)
    for i in range(4):
        for q in range(2):
            far(i, q).wait_send()
    for cond, copy in pending:
        if cond is None:
            copy.wait_send()
        else:
            pl.when(cond)(copy.wait_send)


def per_device(cotangent, down_weight, gate_pre, up_pre):
    groups = lax.axis_size("dp")
    lt, bw = gate_pre.shape
    sw = bw // groups
    tokens = lt * groups
    tile_rows = bw * sw // 128
    vm, dma = pltpu.VMEM, pltpu.SemaphoreType.DMA
    out = pl.pallas_call(
        kernel,
        out_shape=vm((33, 2 * tile_rows, 128), BF16),
        in_specs=[pl.BlockSpec(memory_space=pltpu.VMEM)] * 4,
        out_specs=pl.BlockSpec(memory_space=pltpu.VMEM),
        scratch_shapes=[
            vm((4, 16, lt, 128), BF16),
            vm((4, 4, sw, lt), BF16),
            vm((4, 4, sw, lt), F32),
            vm((4, 4, sw, lt), BF16),
            vm((2, 4, sw, lt), BF16),
            vm((4, 4, 2, sw, lt), BF16),
            vm((2, 4, 128, tokens), BF16),
            vm((2, 4, 37, 128, lt), BF16),
            vm((2, 2 * tile_rows + 32, 128), F32),
            dma((320,)), dma((4,)), dma((4, 16)), dma((2, 4)), dma((4, 4)), dma((4, 4)), dma((4, 37)),
            dma(()),
        ],
        compiler_params=pltpu.CompilerParams(collective_id=0, has_side_effects=True, vmem_limit_bytes=50 << 20),
    )(cotangent, down_weight, gate_pre.T, up_pre.T)
    out = out.reshape(33, tile_rows, 2, 128)
    out = jnp.transpose(out, (2, 0, 1, 3)).reshape(2, 33, bw * sw)
    return out[None, :, :, None, :]


def solution(mesh):
    placed = (P("dp", "tensor"), P("tensor", "dp"), P("dp", "tensor"), P("dp", "tensor"))
    return jax.shard_map(
        per_device,
        mesh=mesh,
        in_specs=placed,
        out_specs=P("tensor", None, None, "dp", None),
        check_vma=False,
    )
```

```python
import jax
import jax.numpy as jnp
from jax import lax
from jax.experimental import pallas as pl
from jax.experimental.pallas import tpu as pltpu
from jax.sharding import PartitionSpec as P

MESH = pl.DeviceIdType.MESH
NT = (((1,), (1,)), ((), ()))
F32 = jnp.float32
BF16 = jnp.bfloat16


def kernel(c_ref, w_ref, gate_ref, up_ref, y_ref,
           cq, hp, hf, hr, gu, rows, grouped, blocks, held, stage,
           s_send, s_cin, s_c, s_gu, s_h, s_rows, s_blk, s_loc):
    t = lax.axis_index("tensor")
    g = lax.axis_index("dp")
    core = t % 2
    y = (t // 2) % 4
    x = (t // 8) % 4
    zl = t // 32
    lt = c_ref.shape[0]
    sw = hp.shape[2]
    tokens = 4 * lt
    inv = 1.0 / tokens

    def tid(zz, xx, yy, cc):
        return ((zz * 4 + xx) * 4 + yy) * 2 + cc

    xp, xm = (x + 1) % 4, (x + 3) % 4
    yp, ym, y2 = (y + 1) % 4, (y + 3) % 4, (y + 2) % 4
    d_xp, d_xm = (tid(zl, xp, y, core), g), (tid(zl, xm, y, core), g)
    d_yp, d_ym = (tid(zl, x, yp, core), g), (tid(zl, x, ym, core), g)
    d_sib = (tid(zl, x, y, 1 - core), g)
    d_z = (tid(1 - zl, x, y, core), g)
    gp, gm, g2 = (g + 1) % 4, (g + 3) % 4, (g + 2) % 4
    d_gp, d_gm, d_g2 = (t, gp), (t, gm), (t, g2)
    d_zg = [(tid(1 - zl, x, y, core), q) for q in (gp, gm, g2)]

    barrier = pltpu.get_barrier_semaphore()
    friends = [d_xp, d_xm, d_yp, d_ym, d_sib, d_z, d_gp, d_gm, d_g2] + d_zg
    for d in friends:
        pl.semaphore_signal(barrier, inc=1, device_id=d, device_id_type=MESH)
    pl.semaphore_wait(barrier, len(friends))

    pending = []

    def send(src, dst, sem, dev, cond=None):
        copy = pltpu.make_async_remote_copy(
            src_ref=src, dst_ref=dst, send_sem=s_send.at[len(pending)], recv_sem=sem,
            device_id=dev, device_id_type=MESH)
        if cond is None:
            copy.start()
        else:
            pl.when(cond)(copy.start)
        pending.append((cond, copy))

    def arrived(ref, sem, cond=None):
        wait = pltpu.make_async_copy(ref, ref, sem).wait
        if cond is None:
            wait()
        else:
            pl.when(cond)(wait)

    home = t // 16
    slot = t % 16
    for p in range(2):
        me = (zl == p) & (home == g)
        dst = cq.at[g, slot]
        send(c_ref, dst, s_cin.at[g], (p * 32 + t % 32, home), jnp.logical_not(me))

        @pl.when(me)
        def _():
            own = pltpu.make_async_copy(c_ref, dst, s_loc)
            own.start()
            own.wait()

    def send_gate_up():
        for q, d in ((g2, d_g2), (gp, d_gp), (gm, d_gm)):
            for i, ref in enumerate((gate_ref, up_ref)):
                send(ref.at[pl.ds(q * sw, sw)], gu.at[i, g], s_gu.at[i, g], d)

    rel = (x + 4 - 2 * (g % 2)) % 4
    owner = rel < 2
    first = jnp.where((rel == 0) | (rel == 3), 0, 1)
    second = 1 - first

    def cslot(col, yy):
        return col * 8 + yy * 2 + core

    def c_send(q, j, dev, cond=None):
        send(cq.at[q, j], cq.at[q, j], s_c.at[q, j], dev, cond)

    def c_got(q, j, cond=None):
        arrived(cq.at[q, j], s_c.at[q, j], cond)

    def c_spread(q, j):
        c_send(q, j, d_yp)
        c_send(q, j, d_ym)
        c_send(q, j, d_sib)

    j1, j2 = cslot(first, y), cslot(second, y)

    def c0(q):
        mine = (zl == g // 2) & (g == q)
        arrived(cq.at[q, slot], s_cin.at[q], owner & jnp.logical_not(mine))
        c_got(q, j1, jnp.logical_not(owner))
        c_send(q, j1, d_xp, rel != 3)
        c_send(q, j1, d_xm, rel != 2)
        c_spread(q, j1)

    def c1(q):
        c_got(q, j2)
        c_spread(q, j2)

    def c_hop(q, col):
        j = cslot(col, ym)
        c_got(q, j)
        c_send(q, j, d_yp, col == 0)
        c_send(q, j, d_sib)
        j = cslot(col, yp)
        c_got(q, j)
        c_send(q, j, d_ym, col == 1)
        c_send(q, j, d_sib)

    def c2(q):
        c_hop(q, first)

    def c3(q):
        c_hop(q, second)

    def c4(q):
        for col in range(2):
            j = cslot(col, y2)
            c_got(q, j)
            c_send(q, j, d_sib)

    def partial(q):
        for i in range(8):
            c_got(q, i * 2 + 1 - core)
        right = jnp.concatenate([cq[q, j] for j in range(16)], axis=1)
        product = lax.dot_general(w_ref[...], right, NT, preferred_element_type=F32)
        for s in range(4):
            part = product[s * sw:(s + 1) * sw]
            hf[q, s] = part
            hp[s, q] = part.astype(BF16)
        for s, d in ((g2, d_g2), (gp, d_gp), (gm, d_gm)):
            send(hp.at[s, q], hr.at[g, q], s_h.at[g, q], d)

    def gradients(q):
        if q == 0:
            for s in (gp, gm, g2):
                for i in range(2):
                    arrived(gu.at[i, s], s_gu.at[i, s])
            own = pl.ds(pl.multiple_of(g * sw, 16), sw)
            gu[0, g] = gate_ref[own, :]
            gu[1, g] = up_ref[own, :]
        for s in (gp, gm, g2):
            arrived(hr.at[s, q], s_h.at[s, q])
        total = hf[q, g]
        for s in (gp, gm, g2):
            total = total + hr[s, q].astype(F32)
        gate = gu[0, q].astype(F32)
        up = gu[1, q].astype(F32)
        sig = jax.nn.sigmoid(gate)
        grads = (total * up * sig * (1.0 + gate * (1.0 - sig)), total * gate * sig)
        for f in range(2):
            value = grads[f].astype(BF16)
            rows[q, g, f] = value
            blocks[f, q, 0, 0:sw] = value

    def unit(q, m):
        return blocks.at[:, q, m, 0:sw]

    def pass_on(q, m_from, dev, m_to, cond=None):
        send(unit(q, m_from), unit(q, m_to), s_blk.at[q, m_to], dev, cond)

    def got(q, m, cond=None):
        arrived(unit(q, m), s_blk.at[q, m], cond)

    def to_sibling(q, m, cond=None):
        pass_on(q, m, d_sib, 17 if isinstance(m, int) and m == 16 else 18 + m, cond)

    def ahead(q, p):
        return (p != 2) if q % 2 == 0 else (p == 1)

    def behind(q, p):
        return (p == 2) if q % 2 == 0 else (p != 1)

    dyp, dym = yp - y, ym - y

    def rows_out(q):
        for d in (d_gp, d_gm):
            send(rows.at[q, g], rows.at[q, g], s_rows.at[q, g], d)

    def rows_on(q):
        for s, other, d in ((gm, 0, d_gp), (gp, 1, d_gm)):
            arrived(rows.at[q, s], s_rows.at[q, s])
            if q % 2 == other:
                send(rows.at[q, s], rows.at[q, s], s_rows.at[q, s], d)

    def b0(q):
        pass_on(q, 0, d_z, 16)
        pass_on(q, 0, d_xp, 4, x < 3)
        pass_on(q, 0, d_xm, 12, x == 0)
        pass_on(q, 0, d_yp, (dyp + 16) % 16, y < 3)
        pass_on(q, 0, d_ym, (dym + 16) % 16, y == 0)
        to_sibling(q, 0, core == 0)

    def b1(q):
        got(q, 16)
        pass_on(q, 16, d_xp, 4, x == 3)
        pass_on(q, 16, d_xm, 12, x > 0)
        pass_on(q, 16, d_yp, (dyp + 16) % 16, y == 3)
        pass_on(q, 16, d_ym, (dym + 16) % 16, y > 0)
        to_sibling(q, 16, core == 1)

    def spread_y(q, m):
        pass_on(q, m, d_yp, (m + dyp + 16) % 16)
        pass_on(q, m, d_ym, (m + dym + 16) % 16)
        to_sibling(q, m)

    def b2x(q):
        got(q, 4)
        pass_on(q, 4, d_xp, 8, ahead(q, xm))
        got(q, 12)
        pass_on(q, 12, d_xm, 8, behind(q, xp))

    def b2y(q):
        spread_y(q, 4)
        spread_y(q, 12)

    def b3(q):
        got(q, 8)
        spread_y(q, 8)

    def b4(base):
        def run(q):
            m = (base + y - ym + 16) % 16
            got(q, m)
            if base == 0:
                pass_on(q, m, d_yp, (m + dyp + 16) % 16, ahead(q, ym))
            elif q % 2 == 0:
                pass_on(q, m, d_yp, (m + dyp + 16) % 16)
            to_sibling(q, m)
            m = (base + y - yp + 16) % 16
            got(q, m)
            if base == 0:
                pass_on(q, m, d_ym, (m + dym + 16) % 16, behind(q, yp))
            elif q % 2 == 1:
                pass_on(q, m, d_ym, (m + dym + 16) % 16)
            to_sibling(q, m)
        return run

    def spare(d):
        return 33 + (d + 4) % 4

    def slot_o(d):
        return jnp.where(d > 0, d, spare(d))

    def slot_x(d):
        return jnp.where(d < 0, 16 + d, spare(d))

    def along_x(q, d):
        so, sx = slot_o(d), slot_x(d)
        pass_on(q, jnp.where(x < 3, so, sx), d_xp, (20 + d) % 16)
        pass_on(q, jnp.where(x == 0, so, sx), d_xm, (28 + d) % 16)

    def y0(q):
        pass_on(q, 0, d_z, 16)
        pass_on(q, 0, d_yp, slot_o(dyp))
        pass_on(q, 0, d_ym, slot_o(dym))
        pass_on(q, 0, d_xp, 4, x < 3)
        pass_on(q, 0, d_xm, 12, x == 0)
        to_sibling(q, 0, core == 0)

    def y1(q):
        got(q, 16)
        pass_on(q, 16, d_yp, slot_x(dyp))
        pass_on(q, 16, d_ym, slot_x(dym))
        pass_on(q, 16, d_xp, 4, x == 3)
        pass_on(q, 16, d_xm, 12, x > 0)
        to_sibling(q, 16, core == 1)

    def y_got(q, source, dest, dev, forward):
        d = y - source
        for pick in (slot_o, slot_x):
            got(q, pick(d))
            if forward:
                pass_on(q, pick(d), dev, pick(dest - source))

    def y_use(q, source):
        d = y - source
        along_x(q, d)
        to_sibling(q, (d + 16) % 16)

    def y2f(q):
        y_got(q, ym, yp, d_yp, q % 2 == 0)
        y_got(q, yp, ym, d_ym, q % 2 == 1)

    def y2x(q):
        y_use(q, ym)
        y_use(q, yp)

    def y3(q):
        y_got(q, y2, None, None, False)
        y_use(q, y2)

    def y4(source):
        def run(q):
            d = y - source
            m = (20 + d) % 16
            got(q, m)
            pass_on(q, m, d_xp, (24 + d) % 16, ahead(q, xm))
            to_sibling(q, m)
            m = (28 + d) % 16
            got(q, m)
            pass_on(q, m, d_xm, (24 + d) % 16, behind(q, xp))
            to_sibling(q, m)
        return run

    def y4b(q):
        y4(ym)(q)
        y4(yp)(q)

    def rows_end(q):
        arrived(rows.at[q, g2], s_rows.at[q, g2])

    def start(q):
        gradients(q)
        (b0 if q < 2 else y0)(q)

    lead = [c0, c1, c2, c3, c4, partial]
    for wave in range(12):
        for q in range(4):
            if 0 <= wave - 2 * q < len(lead):
                lead[wave - 2 * q](q)
        if wave == 0:
            send_gate_up()
    start(0)
    start(1)
    start(2)
    start(3)
    b1(0)
    b1(1)
    b2x(0)
    y1(2)
    b2x(1)
    y1(3)
    for q in range(4):
        rows_out(q)
    y2f(2)
    b2y(0)
    y2f(3)
    b2y(1)
    y2x(2)
    b3(0)
    y2x(3)
    b3(1)
    y4(y)(2)
    y4(y)(3)
    b4(0)(0)
    b4(0)(1)
    y3(2)
    y3(3)
    rows_on(0)
    y4b(2)
    b4(4)(0)
    y4b(3)
    b4(4)(1)
    rows_on(1)
    b4(12)(0)
    y4(y2)(2)
    b4(12)(1)
    rows_on(2)
    y4(y2)(3)
    b4(8)(0)
    b4(8)(1)
    rows_on(3)
    for q in range(4):
        rows_end(q)

    per_class = sw // 8
    target = lax.broadcasted_iota(jnp.int32, (128, sw), 0)
    source = lax.broadcasted_iota(jnp.int32, (128, sw), 1)
    pick = ((target % 16 < per_class) & (source == 8 * (target % 16) + target // 16)).astype(BF16)
    for f in range(2):
        for q in range(4):
            for s in range(4):
                moved = jnp.dot(pick, rows[q, s, f], preferred_element_type=F32)
                grouped[f, s, :, q * lt:(q + 1) * lt] = moved.astype(BF16)
    lane = lax.broadcasted_iota(jnp.int32, (16, 128), 1)

    order = (0, 8, 9, 6, 15, 1, 7, 10, 16, 2, 4, 11, 13, 3, 5, 12, 14)

    def pair_of(i):
        p = jnp.int32(0)
        for at, value in enumerate(order):
            p = jnp.where(i == at, value, p)
        return p

    def product(p, f):
        left = grouped[f].reshape(512, tokens)
        right = jnp.concatenate(
            [blocks[f, q, pl.ds(2 * p, 2)].reshape(256, lt) for q in range(4)], axis=1)
        held[f] = lax.dot_general(left, right, NT, preferred_element_type=F32)

    def regroup(f):
        for half in range(2):
            for s in range(4):
                turned = [
                    pltpu.roll(
                        held[f, s * 128 + r * 16:s * 128 + r * 16 + 16, half * 128:half * 128 + 128] * inv,
                        (128 - 16 * r) % 128, 1)
                    for r in range(8)
                ]
                for r in range(7):
                    merged = jnp.where(lane < 112 - 16 * r, turned[r], turned[r + 1])
                    stage[half, pl.ds(14 * per_class * s + 2 * r + f, 16, stride=14), :] = merged

    def put_tiles(p):
        for half in range(2):
            at = 2 * p + half
            k = jnp.where(at < 17, 2 * at, jnp.where(at == 17, 31, 2 * (at - 18) + 2 * core - 1))
            k = jnp.where(k < 0, 1, k)
            y_ref[k] = stage[half, 0:y_ref.shape[1], :].astype(BF16)

    def step(i):
        for f in range(2):
            regroup(f)
            product(pair_of(i), f)
        put_tiles(pair_of(i - 1))

    base_index = len(pending)
    assert base_index + 16 <= s_send.shape[0], base_index

    def last_hop(n, q, m):
        got(q, m)
        pltpu.make_async_remote_copy(
            src_ref=unit(q, m), dst_ref=unit(q, 18 + m), send_sem=s_send.at[base_index + n],
            recv_sem=s_blk.at[q, 18 + m], device_id=d_sib, device_id_type=MESH).start()

    def x_far(source, q):
        at = {id(y): 0, id(ym): 1, id(yp): 2, id(y2): 3}[id(source)]
        last_hop(at * 2 + q - 2, q, (24 + y - source) % 16)

    def y_far():
        for b in range(4):
            for q in range(2):
                last_hop(8 + b * 2 + q, q, 4 * b + 2)

    after = {
        1: [lambda: x_far(y, 2), lambda: x_far(y, 3)], 2: [lambda: x_far(ym, 2)], 3: [lambda: x_far(ym, 3)],
        4: [y_far], 6: [lambda: x_far(yp, 2)], 8: [lambda: x_far(yp, 3)],
        10: [lambda: x_far(y2, 2)], 12: [lambda: x_far(y2, 3)],
    }

    def body(i, _):
        p = pair_of(i)

        @pl.when((p == 8) & (core == 0))
        def _():
            for q in range(4):
                got(q, 17)

        @pl.when(p > 8)
        def _():
            for q in range(4):
                got(q, 2 * p, (p > 9) | (core == 1))
                got(q, 2 * p + 1)

        step(i)
        for at, runs in after.items():
            @pl.when(i == at)
            def _(runs=runs):
                for run in runs:
                    run()
        return 0

    lax.fori_loop(0, 17, body, 0)
    for f in range(2):
        regroup(f)
    put_tiles(pair_of(16))
    for n in range(16):
        pltpu.make_async_remote_copy(
            src_ref=unit(0, 0), dst_ref=unit(0, 0), send_sem=s_send.at[base_index + n],
            recv_sem=s_blk.at[0, 0], device_id=d_sib, device_id_type=MESH).wait_send()
    for cond, copy in pending:
        if cond is None:
            copy.wait_send()
        else:
            pl.when(cond)(copy.wait_send)


def per_device(cotangent, down_weight, gate_pre, up_pre):
    groups = lax.axis_size("dp")
    lt, bw = gate_pre.shape
    sw = bw // groups
    tokens = lt * groups
    tile_rows = bw * sw // 128
    vm, dma = pltpu.VMEM, pltpu.SemaphoreType.DMA
    out = pl.pallas_call(
        kernel,
        out_shape=vm((33, 2 * tile_rows, 128), BF16),
        in_specs=[pl.BlockSpec(memory_space=pltpu.VMEM)] * 4,
        out_specs=pl.BlockSpec(memory_space=pltpu.VMEM),
        scratch_shapes=[
            vm((4, 16, lt, 128), BF16),
            vm((4, 4, sw, lt), BF16),
            vm((4, 4, sw, lt), F32),
            vm((4, 4, sw, lt), BF16),
            vm((2, 4, sw, lt), BF16),
            vm((4, 4, 2, sw, lt), BF16),
            vm((2, 4, 128, tokens), BF16),
            vm((2, 4, 37, 128, lt), BF16),
            vm((2, 512, 256), F32),
            vm((2, 2 * tile_rows + 32, 128), F32),
            dma((320,)), dma((4,)), dma((4, 16)), dma((2, 4)), dma((4, 4)), dma((4, 4)), dma((4, 37)),
            dma(()),
        ],
        compiler_params=pltpu.CompilerParams(collective_id=0, has_side_effects=True, vmem_limit_bytes=50 << 20),
    )(cotangent, down_weight, gate_pre.T, up_pre.T)
    out = out.reshape(33, tile_rows, 2, 128)
    out = jnp.transpose(out, (2, 0, 1, 3)).reshape(2, 33, bw * sw)
    return out[None, :, :, None, :]


def solution(mesh):
    placed = (P("dp", "tensor"), P("tensor", "dp"), P("dp", "tensor"), P("dp", "tensor"))
    return jax.shard_map(
        per_device,
        mesh=mesh,
        in_specs=placed,
        out_specs=P("tensor", None, None, "dp", None),
        check_vma=False,
    )
```

```python
import jax
import jax.numpy as jnp
from jax import lax
from jax.experimental import pallas as pl
from jax.experimental.pallas import tpu as pltpu
from jax.sharding import PartitionSpec as P

MESH = pl.DeviceIdType.MESH
NT = (((1,), (1,)), ((), ()))
F32 = jnp.float32
BF16 = jnp.bfloat16


def kernel(c_ref, w_ref, gate_ref, up_ref, y_ref,
           cq, hp, hf, hr, gu, rows, grouped, blocks, held, stage,
           s_send, s_cin, s_c, s_gu, s_h, s_rows, s_blk, s_loc):
    t = lax.axis_index("tensor")
    g = lax.axis_index("dp")
    core = t % 2
    y = (t // 2) % 4
    x = (t // 8) % 4
    zl = t // 32
    lt = c_ref.shape[0]
    sw = hp.shape[2]
    tokens = 4 * lt
    inv = 1.0 / tokens

    def tid(zz, xx, yy, cc):
        return ((zz * 4 + xx) * 4 + yy) * 2 + cc

    xp, xm = (x + 1) % 4, (x + 3) % 4
    yp, ym, y2 = (y + 1) % 4, (y + 3) % 4, (y + 2) % 4
    d_xp, d_xm = (tid(zl, xp, y, core), g), (tid(zl, xm, y, core), g)
    d_yp, d_ym = (tid(zl, x, yp, core), g), (tid(zl, x, ym, core), g)
    d_sib = (tid(zl, x, y, 1 - core), g)
    d_z = (tid(1 - zl, x, y, core), g)
    gp, gm, g2 = (g + 1) % 4, (g + 3) % 4, (g + 2) % 4
    d_gp, d_gm, d_g2 = (t, gp), (t, gm), (t, g2)
    d_zg = [(tid(1 - zl, x, y, core), q) for q in (gp, gm, g2)]

    barrier = pltpu.get_barrier_semaphore()
    friends = [d_xp, d_xm, d_yp, d_ym, d_sib, d_z, d_gp, d_gm, d_g2] + d_zg
    for d in friends:
        pl.semaphore_signal(barrier, inc=1, device_id=d, device_id_type=MESH)
    pl.semaphore_wait(barrier, len(friends))

    pending = []

    def send(src, dst, sem, dev, cond=None):
        copy = pltpu.make_async_remote_copy(
            src_ref=src, dst_ref=dst, send_sem=s_send.at[len(pending)], recv_sem=sem,
            device_id=dev, device_id_type=MESH)
        if cond is None:
            copy.start()
        else:
            pl.when(cond)(copy.start)
        pending.append((cond, copy))

    def drain(sends):
        for cond, copy in sends:
            if cond is None:
                copy.wait_send()
            else:
                pl.when(cond)(copy.wait_send)

    def arrived(ref, sem, cond=None):
        wait = pltpu.make_async_copy(ref, ref, sem).wait
        if cond is None:
            wait()
        else:
            pl.when(cond)(wait)

    home = t // 16
    slot = t % 16
    for p in range(2):
        me = (zl == p) & (home == g)
        dst = cq.at[g, slot]
        send(c_ref, dst, s_cin.at[g], (p * 32 + t % 32, home), jnp.logical_not(me))

        @pl.when(me)
        def _():
            own = pltpu.make_async_copy(c_ref, dst, s_loc)
            own.start()
            own.wait()

    def send_gate_up():
        for q, d in ((g2, d_g2), (gp, d_gp), (gm, d_gm)):
            for i, ref in enumerate((gate_ref, up_ref)):
                send(ref.at[pl.ds(q * sw, sw)], gu.at[i, g], s_gu.at[i, g], d)

    rel = (x + 4 - 2 * (g % 2)) % 4
    owner = rel < 2
    first = jnp.where((rel == 0) | (rel == 3), 0, 1)
    second = 1 - first

    def cslot(col, yy):
        return col * 8 + yy * 2 + core

    def c_send(q, j, dev, cond=None):
        send(cq.at[q, j], cq.at[q, j], s_c.at[q, j], dev, cond)

    def c_got(q, j, cond=None):
        arrived(cq.at[q, j], s_c.at[q, j], cond)

    def c_spread(q, j):
        c_send(q, j, d_yp)
        c_send(q, j, d_ym)
        c_send(q, j, d_sib)

    j1, j2 = cslot(first, y), cslot(second, y)

    def c0(q):
        mine = (zl == g // 2) & (g == q)
        arrived(cq.at[q, slot], s_cin.at[q], owner & jnp.logical_not(mine))
        c_got(q, j1, jnp.logical_not(owner))
        c_send(q, j1, d_xp, rel != 3)
        c_send(q, j1, d_xm, rel != 2)
        c_spread(q, j1)

    def c1(q):
        c_got(q, j2)
        c_spread(q, j2)

    def c_hop(q, col):
        j = cslot(col, ym)
        c_got(q, j)
        c_send(q, j, d_yp, col == 0)
        c_send(q, j, d_sib)
        j = cslot(col, yp)
        c_got(q, j)
        c_send(q, j, d_ym, col == 1)
        c_send(q, j, d_sib)

    def c2(q):
        c_hop(q, first)

    def c3(q):
        c_hop(q, second)

    def c4(q):
        for col in range(2):
            j = cslot(col, y2)
            c_got(q, j)
            c_send(q, j, d_sib)

    def partial(q):
        for i in range(8):
            c_got(q, i * 2 + 1 - core)
        right = jnp.concatenate([cq[q, j] for j in range(16)], axis=1)
        product = lax.dot_general(w_ref[...], right, NT, preferred_element_type=F32)
        for s in range(4):
            part = product[s * sw:(s + 1) * sw]
            hf[q, s] = part
            hp[s, q] = part.astype(BF16)
        for s, d in ((g2, d_g2), (gp, d_gp), (gm, d_gm)):
            send(hp.at[s, q], hr.at[g, q], s_h.at[g, q], d)

    def gradients(q):
        if q == 0:
            for s in (gp, gm, g2):
                for i in range(2):
                    arrived(gu.at[i, s], s_gu.at[i, s])
            own = pl.ds(pl.multiple_of(g * sw, 16), sw)
            gu[0, g] = gate_ref[own, :]
            gu[1, g] = up_ref[own, :]
        for s in (gp, gm, g2):
            arrived(hr.at[s, q], s_h.at[s, q])
        total = hf[q, g]
        for s in (gp, gm, g2):
            total = total + hr[s, q].astype(F32)
        gate = gu[0, q].astype(F32)
        up = gu[1, q].astype(F32)
        sig = jax.nn.sigmoid(gate)
        grads = (total * up * sig * (1.0 + gate * (1.0 - sig)), total * gate * sig)
        for f in range(2):
            value = grads[f].astype(BF16)
            rows[q, g, f] = value
            blocks[f, q, 0, 0:sw] = value

    def unit(q, m):
        return blocks.at[:, q, m, 0:sw]

    def pass_on(q, m_from, dev, m_to, cond=None):
        send(unit(q, m_from), unit(q, m_to), s_blk.at[q, m_to], dev, cond)

    def got(q, m, cond=None):
        arrived(unit(q, m), s_blk.at[q, m], cond)

    def to_sibling(q, m, cond=None):
        pass_on(q, m, d_sib, 17 if isinstance(m, int) and m == 16 else 18 + m, cond)

    def ahead(q, p):
        return (p != 2) if q % 2 == 0 else (p == 1)

    def behind(q, p):
        return (p == 2) if q % 2 == 0 else (p != 1)

    dyp, dym = yp - y, ym - y

    def rows_out(q):
        for d in (d_gp, d_gm):
            send(rows.at[q, g], rows.at[q, g], s_rows.at[q, g], d)

    def rows_on(q):
        for s, other, d in ((gm, 0, d_gp), (gp, 1, d_gm)):
            arrived(rows.at[q, s], s_rows.at[q, s])
            if q % 2 == other:
                send(rows.at[q, s], rows.at[q, s], s_rows.at[q, s], d)

    def b0(q):
        pass_on(q, 0, d_z, 16)
        pass_on(q, 0, d_xp, 4, x < 3)
        pass_on(q, 0, d_xm, 12, x == 0)
        pass_on(q, 0, d_yp, (dyp + 16) % 16, y < 3)
        pass_on(q, 0, d_ym, (dym + 16) % 16, y == 0)
        to_sibling(q, 0, core == 0)

    def b1(q):
        got(q, 16)
        pass_on(q, 16, d_xp, 4, x == 3)
        pass_on(q, 16, d_xm, 12, x > 0)
        pass_on(q, 16, d_yp, (dyp + 16) % 16, y == 3)
        pass_on(q, 16, d_ym, (dym + 16) % 16, y > 0)
        to_sibling(q, 16, core == 1)

    def spread_y(q, m):
        pass_on(q, m, d_yp, (m + dyp + 16) % 16)
        pass_on(q, m, d_ym, (m + dym + 16) % 16)
        to_sibling(q, m)

    def b2x(q):
        got(q, 4)
        pass_on(q, 4, d_xp, 8, ahead(q, xm))
        got(q, 12)
        pass_on(q, 12, d_xm, 8, behind(q, xp))

    def b2y(q):
        spread_y(q, 4)
        spread_y(q, 12)

    def b3(q):
        got(q, 8)
        spread_y(q, 8)

    def b4(base):
        def run(q):
            m = (base + y - ym + 16) % 16
            got(q, m)
            if base == 0:
                pass_on(q, m, d_yp, (m + dyp + 16) % 16, ahead(q, ym))
            elif q % 2 == 0:
                pass_on(q, m, d_yp, (m + dyp + 16) % 16)
            to_sibling(q, m)
            m = (base + y - yp + 16) % 16
            got(q, m)
            if base == 0:
                pass_on(q, m, d_ym, (m + dym + 16) % 16, behind(q, yp))
            elif q % 2 == 1:
                pass_on(q, m, d_ym, (m + dym + 16) % 16)
            to_sibling(q, m)
        return run

    def spare(d):
        return 33 + (d + 4) % 4

    def slot_o(d):
        return jnp.where(d > 0, d, spare(d))

    def slot_x(d):
        return jnp.where(d < 0, 16 + d, spare(d))

    def along_x(q, d):
        so, sx = slot_o(d), slot_x(d)
        pass_on(q, jnp.where(x < 3, so, sx), d_xp, (20 + d) % 16)
        pass_on(q, jnp.where(x == 0, so, sx), d_xm, (28 + d) % 16)

    def y0(q):
        pass_on(q, 0, d_z, 16)
        pass_on(q, 0, d_yp, slot_o(dyp))
        pass_on(q, 0, d_ym, slot_o(dym))
        pass_on(q, 0, d_xp, 4, x < 3)
        pass_on(q, 0, d_xm, 12, x == 0)
        to_sibling(q, 0, core == 0)

    def y1(q):
        got(q, 16)
        pass_on(q, 16, d_yp, slot_x(dyp))
        pass_on(q, 16, d_ym, slot_x(dym))
        pass_on(q, 16, d_xp, 4, x == 3)
        pass_on(q, 16, d_xm, 12, x > 0)
        to_sibling(q, 16, core == 1)

    def y_got(q, source, dest, dev, forward):
        d = y - source
        for pick in (slot_o, slot_x):
            got(q, pick(d))
            if forward:
                pass_on(q, pick(d), dev, pick(dest - source))

    def y_use(q, source):
        d = y - source
        along_x(q, d)
        to_sibling(q, (d + 16) % 16)

    def y2f(q):
        y_got(q, ym, yp, d_yp, q % 2 == 0)
        y_got(q, yp, ym, d_ym, q % 2 == 1)

    def y2x(q):
        y_use(q, ym)
        y_use(q, yp)

    def y3(q):
        y_got(q, y2, None, None, False)
        y_use(q, y2)

    def y4(source):
        def run(q):
            d = y - source
            m = (20 + d) % 16
            got(q, m)
            pass_on(q, m, d_xp, (24 + d) % 16, ahead(q, xm))
            to_sibling(q, m)
            m = (28 + d) % 16
            got(q, m)
            pass_on(q, m, d_xm, (24 + d) % 16, behind(q, xp))
            to_sibling(q, m)
        return run

    def y4b(q):
        y4(ym)(q)
        y4(yp)(q)

    def rows_end(q):
        arrived(rows.at[q, g2], s_rows.at[q, g2])

    def start(q):
        gradients(q)
        (b0 if q < 2 else y0)(q)

    lead = [c0, c1, c2, c3, c4, partial]
    for wave in range(12):
        for q in range(4):
            if 0 <= wave - 2 * q < len(lead):
                lead[wave - 2 * q](q)
        if wave == 0:
            send_gate_up()
    start(0)
    start(1)
    start(2)
    start(3)
    b1(0)
    b1(1)
    b2x(0)
    y1(2)
    b2x(1)
    y1(3)
    for q in range(4):
        rows_out(q)
    y2f(2)
    b2y(0)
    y2f(3)
    b2y(1)
    y2x(2)
    b3(0)
    y2x(3)
    b3(1)
    y4(y)(2)
    y4(y)(3)
    b4(0)(0)
    b4(0)(1)
    y3(2)
    y3(3)
    rows_on(0)
    y4b(2)
    b4(4)(0)
    y4b(3)
    b4(4)(1)
    rows_on(1)
    b4(12)(0)
    rows_on(2)
    y4(y2)(2)
    b4(12)(1)
    y4(y2)(3)
    b4(8)(0)
    b4(8)(1)
    rows_on(3)
    sent = len(pending) - 40
    drain(pending[:sent])
    for q in range(4):
        rows_end(q)

    per_class = sw // 8
    target = lax.broadcasted_iota(jnp.int32, (128, sw), 0)
    source = lax.broadcasted_iota(jnp.int32, (128, sw), 1)
    pick = ((target % 16 < per_class) & (source == 8 * (target % 16) + target // 16)).astype(BF16)
    for f in range(2):
        for q in range(4):
            for s in range(4):
                moved = jnp.dot(pick, rows[q, s, f], preferred_element_type=F32)
                grouped[f, s, :, q * lt:(q + 1) * lt] = moved.astype(BF16)
    lane = lax.broadcasted_iota(jnp.int32, (16, 128), 1)

    order = (0, 8, 9, 6, 15, 1, 7, 10, 16, 2, 4, 11, 13, 3, 5, 12, 14)

    def pair_of(i):
        p = jnp.int32(0)
        for at, value in enumerate(order):
            p = jnp.where(i == at, value, p)
        return p

    def product(p, f):
        left = grouped[f].reshape(512, tokens)
        right = jnp.concatenate(
            [blocks[f, q, pl.ds(2 * p, 2)].reshape(256, lt) for q in range(4)], axis=1)
        held[f] = lax.dot_general(left, right, NT, preferred_element_type=F32)

    def regroup(f):
        for half in range(2):
            for s in range(4):
                turned = [
                    pltpu.roll(
                        held[f, s * 128 + r * 16:s * 128 + r * 16 + 16, half * 128:half * 128 + 128] * inv,
                        (128 - 16 * r) % 128, 1)
                    for r in range(8)
                ]
                for r in range(7):
                    merged = jnp.where(lane < 112 - 16 * r, turned[r], turned[r + 1])
                    stage[half, pl.ds(14 * per_class * s + 2 * r + f, 16, stride=14), :] = merged

    def put_tiles(p):
        for half in range(2):
            at = 2 * p + half
            k = jnp.where(at < 17, 2 * at, jnp.where(at == 17, 31, 2 * (at - 18) + 2 * core - 1))
            k = jnp.where(k < 0, 1, k)
            y_ref[k] = stage[half, 0:y_ref.shape[1], :].astype(BF16)

    def step(i):
        put_tiles(pair_of(i - 2))
        for f in range(2):
            regroup(f)
            product(pair_of(i), f)

    base_index = len(pending)
    assert base_index + 16 <= s_send.shape[0], base_index

    def last_hop(n, q, m):
        got(q, m)
        pltpu.make_async_remote_copy(
            src_ref=unit(q, m), dst_ref=unit(q, 18 + m), send_sem=s_send.at[base_index + n],
            recv_sem=s_blk.at[q, 18 + m], device_id=d_sib, device_id_type=MESH).start()

    def x_far(source, q):
        at = {id(y): 0, id(ym): 1, id(yp): 2, id(y2): 3}[id(source)]
        last_hop(at * 2 + q - 2, q, (24 + y - source) % 16)

    def y_far():
        for b in range(4):
            for q in range(2):
                last_hop(8 + b * 2 + q, q, 4 * b + 2)

    after = {
        1: [lambda: x_far(y, 2), lambda: x_far(y, 3)], 2: [lambda: x_far(ym, 2)], 3: [lambda: x_far(ym, 3)],
        4: [y_far], 6: [lambda: x_far(yp, 2)], 8: [lambda: x_far(yp, 3)],
        10: [lambda: x_far(y2, 2)], 12: [lambda: x_far(y2, 3)],
    }

    def body(i, _):
        p = pair_of(i)

        @pl.when((p == 8) & (core == 0))
        def _():
            for q in range(4):
                got(q, 17)

        @pl.when(p > 8)
        def _():
            for q in range(4):
                got(q, 2 * p, (p > 9) | (core == 1))
                got(q, 2 * p + 1)

        step(i)
        for at, runs in after.items():
            @pl.when(i == at)
            def _(runs=runs):
                for run in runs:
                    run()
        return 0

    lax.fori_loop(0, 17, body, 0)
    put_tiles(pair_of(15))
    for f in range(2):
        regroup(f)
    put_tiles(pair_of(16))
    for n in range(16):
        pltpu.make_async_remote_copy(
            src_ref=unit(0, 0), dst_ref=unit(0, 0), send_sem=s_send.at[base_index + n],
            recv_sem=s_blk.at[0, 0], device_id=d_sib, device_id_type=MESH).wait_send()
    drain(pending[sent:])


def per_device(cotangent, down_weight, gate_pre, up_pre):
    groups = lax.axis_size("dp")
    lt, bw = gate_pre.shape
    sw = bw // groups
    tokens = lt * groups
    tile_rows = bw * sw // 128
    vm, dma = pltpu.VMEM, pltpu.SemaphoreType.DMA
    out = pl.pallas_call(
        kernel,
        out_shape=vm((33, 2 * tile_rows, 128), BF16),
        in_specs=[pl.BlockSpec(memory_space=pltpu.VMEM)] * 4,
        out_specs=pl.BlockSpec(memory_space=pltpu.VMEM),
        scratch_shapes=[
            vm((4, 16, lt, 128), BF16),
            vm((4, 4, sw, lt), BF16),
            vm((4, 4, sw, lt), F32),
            vm((4, 4, sw, lt), BF16),
            vm((2, 4, sw, lt), BF16),
            vm((4, 4, 2, sw, lt), BF16),
            vm((2, 4, 128, tokens), BF16),
            vm((2, 4, 37, 128, lt), BF16),
            vm((2, 512, 256), F32),
            vm((2, 2 * tile_rows + 32, 128), F32),
            dma((320,)), dma((4,)), dma((4, 16)), dma((2, 4)), dma((4, 4)), dma((4, 4)), dma((4, 37)),
            dma(()),
        ],
        compiler_params=pltpu.CompilerParams(collective_id=0, has_side_effects=True, vmem_limit_bytes=50 << 20),
    )(cotangent, down_weight, gate_pre.T, up_pre.T)
    out = out.reshape(33, tile_rows, 2, 128)
    out = jnp.transpose(out, (2, 0, 1, 3)).reshape(2, 33, bw * sw)
    return out[None, :, :, None, :]


def solution(mesh):
    placed = (P("dp", "tensor"), P("tensor", "dp"), P("dp", "tensor"), P("dp", "tensor"))
    return jax.shard_map(
        per_device,
        mesh=mesh,
        in_specs=placed,
        out_specs=P("tensor", None, None, "dp", None),
        check_vma=False,
    )
```
